32 devices in a mesh: band: 4 (over x, core), slab: 8 (over z, y).
Axes of the slice: x: 2, y: 2, z: 4, core: 2. Of those that a mesh axis runs over, the one named last changes fastest.
Arguments:
- resident: float32 [8, 128, 128, 128], P('band', 'slab'), may hold values from -5 to 5
- blocks: float32 [16, 128, 128, 128], P('band', 'slab'), may hold values from -5 to 5
- occupation: float32 [16], replicated, may hold values from 0.25 to 1
Outputs:
- exchange_term: float32 [8, 128, 128, 128], P('band', 'slab')
The draws below stay inside these ranges and needn't reach their ends.
All inputs are finite; a program needn't handle non-finite values.
Results may differ from the reference program's by a relative error of at most 0.0001.
Values sent between devices are 32-bit elements; how exact they have to be, the bound alone decides.
No kernel may reach another device: no remote copies, remote signals or barrier semaphores. Data moves between devices by JAX's collectives and lax.ppermute only.
A program may use at most 192 MiB of HBM per device.

```python
import math
import jax
import jax.numpy as jnp
from jax import lax

GRID = 128
SRC = 16
ORBS = 8


def shard_levels(key, dims, split, smallest, high):
    gain, own = 1.0, jax.random.fold_in(key, 6)
    for dim, shards_of in split:
        steps = jnp.exp(jax.random.uniform(jax.random.fold_in(own, dim), (shards_of,), jnp.float32, smallest / len(split), high / len(split)))
        gain = gain * jnp.repeat(steps, dims[dim] // shards_of).reshape([-1 if axis == dim else 1 for axis in range(len(dims))])
    return gain


def bell_draw(rng, dims, spread, limit, pieces=(), held_as=jnp.bfloat16):
    result = spread * jax.random.normal(rng, dims, jnp.float32)
    if pieces:
        result = result * shard_levels(rng, dims, pieces, -0.22, 0.18)
    return jnp.clip(result, -limit, limit).astype(held_as)


def setup_inputs(seed: int = 0) -> dict:
    key_of = jax.random.split(jax.random.key(seed), 4)
    return {
        "resident": bell_draw(key_of[0], (ORBS, GRID, GRID, GRID), 0.35, 5.0, ((0, 4), (1, 8)), jnp.float32),
        "blocks": bell_draw(key_of[1], (SRC, GRID, GRID, GRID), 0.35, 5.0, ((0, 4), (1, 8)), jnp.float32),
        "occupation": jnp.clip(jnp.exp(jax.random.uniform(key_of[2], (SRC,), jnp.float32, math.log(0.25), math.log(1.0))), 0.25, 1.0),
    }


KAPPA_SQ = 0.01


def wave_numbers(grid_len):
    freqs = jnp.fft.fftfreq(grid_len) * (2.0 * math.pi)
    return freqs.astype(jnp.float32)


def coulomb_kernel():
    waves = wave_numbers(GRID)
    squared = waves[:, None, None] ** 2 + waves[None, :, None] ** 2 + waves[None, None, :] ** 2
    return (4.0 * math.pi) / (squared + KAPPA_SQ)


def reference(resident, blocks, occupation):
    source = blocks
    kernel = coulomb_kernel()

    def one_orbital(orbital):
        def accumulate(running, inputs):
            block_orb, weight = inputs
            density = orbital * block_orb
            potential = jnp.fft.ifftn(kernel * jnp.fft.fftn(density)).real.astype(jnp.float32)
            return running - weight * potential * block_orb, None

        running, _ = lax.scan(accumulate, jnp.zeros_like(orbital), (source, occupation))
        return running

    return lax.map(one_orbital, resident)
```

```python
import functools
import math

import jax
import jax.numpy as jnp
from jax import lax
from jax.experimental import pallas as pl
from jax.experimental.pallas import tpu as pltpu
from jax.sharding import PartitionSpec as P

KAPPA_SQ = 0.01
F32, BF16 = (jnp.float32, jnp.bfloat16)


def dft_tables(grid_len):
    indices = jnp.arange(grid_len, dtype=jnp.int32)
    product = indices[:, None] * indices[None, :] % grid_len
    angles = product.astype(jnp.float32) * (2.0 * math.pi / grid_len)
    return (jnp.cos(angles), jnp.sin(angles))


def transform(real_part, imag_part, form, cos_t, sin_t, sign_val):

    def apply(values, table):
        return jnp.einsum(
            form, values, table, precision=lax.Precision.HIGHEST, preferred_element_type=jnp.float32
        )

    real_cos = apply(real_part, cos_t)
    real_sin = apply(real_part, sin_t)
    imag_cos = apply(imag_part, cos_t)
    imag_sin = apply(imag_part, sin_t)
    return (real_cos - sign_val * imag_sin, imag_cos + sign_val * real_sin)


def wave_of(indices, grid_len):
    signed = jnp.where(indices > (grid_len - 1) // 2, indices - grid_len, indices)
    return signed.astype(jnp.float32) * (2.0 * math.pi / grid_len)


def coulomb(wave_z, wave_y, wave_x):
    squared = wave_z[:, None, None] ** 2 + wave_y[None, :, None] ** 2 + wave_x[None, None, :] ** 2
    return 4.0 * math.pi / (squared + KAPPA_SQ)


def sliced_grids(resident, blocks, occupation):
    orb_count, plane_count, grid_len, _ = resident.shape
    local_src = blocks.shape[0]
    group_count = lax.axis_size("band")
    src_count = local_src * group_count
    cos_t, sin_t = dft_tables(grid_len)
    along_x = "fzyx,xk->fzyk"
    along_y = "fzyx,yk->fzkx"
    along_z = "fzyx,zk->fkyx"
    source = lax.all_gather(blocks, "band", axis=0, tiled=True)
    count_pairs = source.shape[0] // 2
    even_src = source[0::2]
    odd_src = source[1::2]
    real_part = (resident[:, None] * even_src[None]).reshape(
        orb_count * count_pairs, plane_count, grid_len, grid_len
    )
    imag_part = (resident[:, None] * odd_src[None]).reshape(
        orb_count * count_pairs, plane_count, grid_len, grid_len
    )
    real_part, imag_part = transform(real_part, imag_part, along_x, cos_t, sin_t, -1.0)
    real_part, imag_part = transform(real_part, imag_part, along_y, cos_t, sin_t, -1.0)
    shaped = (orb_count, count_pairs, plane_count, grid_len, grid_len)
    real_part, imag_part = (real_part.reshape(shaped), imag_part.reshape(shaped))
    field_count = orb_count * (src_count // 2)
    flat = (field_count, plane_count, grid_len, grid_len)
    real_part = real_part.reshape(flat)
    imag_part = imag_part.reshape(flat)
    all_waves = wave_of(jnp.arange(grid_len, dtype=jnp.int32), grid_len)
    position = lax.axis_index("slab")
    col_real = lax.all_to_all(real_part, "slab", split_axis=2, concat_axis=1, tiled=True)
    col_imag = lax.all_to_all(imag_part, "slab", split_axis=2, concat_axis=1, tiled=True)
    width_y = col_real.shape[2]
    local_waves = wave_of(position * width_y + jnp.arange(width_y, dtype=jnp.int32), grid_len)
    kernel = coulomb(all_waves, local_waves, all_waves)
    col_real, col_imag = transform(col_real, col_imag, along_z, cos_t, sin_t, -1.0)
    col_real = col_real * kernel[None]
    col_imag = col_imag * kernel[None]
    col_real, col_imag = transform(col_real, col_imag, along_z, cos_t, sin_t, 1.0)
    real_part = lax.all_to_all(col_real, "slab", split_axis=1, concat_axis=2, tiled=True)
    imag_part = lax.all_to_all(col_imag, "slab", split_axis=1, concat_axis=2, tiled=True)
    real_part, imag_part = transform(real_part, imag_part, along_y, cos_t, sin_t, 1.0)
    real_part, imag_part = transform(real_part, imag_part, along_x, cos_t, sin_t, 1.0)
    scale_inv = 1.0 / float(grid_len * grid_len * grid_len)
    shaped = (orb_count, src_count // 2, plane_count, grid_len, grid_len)
    pot_even = real_part.reshape(shaped) * scale_inv
    pot_odd = imag_part.reshape(shaped) * scale_inv
    weighted_even = source[0::2] * occupation[0::2][:, None, None, None]
    weighted_odd = source[1::2] * occupation[1::2][:, None, None, None]
    summed = jnp.sum(pot_even * weighted_even[None], axis=1) + jnp.sum(
        pot_odd * weighted_odd[None], axis=1
    )
    return -summed


def halves(value):
    top = value.astype(BF16)
    return (top, (value - top.astype(F32)).astype(BF16))


def cas_tables(grid_len):
    indices = jnp.arange(grid_len, dtype=jnp.int32)
    product = indices[:, None] * indices[None, :] % grid_len
    angles = product.astype(F32) * (2.0 * math.pi / grid_len)
    table = jnp.cos(angles) + jnp.sin(angles)
    top = lax.reduce_precision(table, 8, 7)
    high, low = (top.astype(BF16), (table - top).astype(BF16))
    zero = jnp.zeros_like(high)
    right = jnp.block([[high, low], [high, zero]])
    left = jnp.block([[high, high], [low, zero]])
    return (right, left)


def times_table(rows, right):
    grid_len = rows.shape[1]
    both = jnp.dot(jnp.concatenate(halves(rows), 1), right, preferred_element_type=F32)
    return both[:, :grid_len] + both[:, grid_len:]


def table_times(left, cols):
    grid_len = cols.shape[0]
    both = jnp.dot(left, jnp.concatenate(halves(cols), 0), preferred_element_type=F32)
    return both[:grid_len] + both[grid_len:]


def beside(rows, count):
    size = rows.shape[0] // count
    return jnp.concatenate([rows[k * size : (k + 1) * size] for k in range(count)], 1)


def below(cols, count):
    size = cols.shape[1] // count
    return jnp.concatenate([cols[:, k * size : (k + 1) * size] for k in range(count)], 0)


STEP = 16


def exchange_kernel(grid_len, slots, first, where_ref, occ_ref, gx_ref, gz_ref, right_ref, left_ref, *refs):
    refs = list(refs)
    res_refs = [refs.pop(0) for _ in range(2 * slots - 1)]
    src_refs = [refs.pop(0) for _ in range(4)]
    old_refs = [] if first else [refs.pop(0) for _ in range(slots)]
    out_refs = [refs.pop(0) for _ in range(slots)]
    res, src, work, acc, res_sem, src_sem, old_sem, out_sem = refs
    n = grid_len
    slot_len = n // slots
    slab_len = slot_len // 2
    slabs = 2 * slots
    place = where_ref[8]

    def res_copy(ref, slot):
        return pltpu.make_async_copy(ref, res.at[pl.ds(slot * slot_len, slot_len)], res_sem.at[slot])

    def src_copy(ref, slab):
        return pltpu.make_async_copy(ref, src.at[pl.ds(slab * slab_len, slab_len)], src_sem.at[slab])

    def old_copy(slot):
        return pltpu.make_async_copy(old_refs[slot], acc.at[pl.ds(slot * slot_len, slot_len)], old_sem.at[slot])

    def out_copy(slot):
        return pltpu.make_async_copy(acc.at[pl.ds(slot * slot_len, slot_len)], out_refs[slot], out_sem.at[slot])

    res_copy(res_refs[0], 0).start()
    for k in range(4):
        for half in range(2):
            src_copy(src_refs[k].at[half], where_ref[2 * k + half]).start()
    for slot in range(1, slots):
        down, up = (res_refs[slot], res_refs[slots - 1 + slots - slot])

        @pl.when(place + slot < slots)
        def _(down=down, slot=slot):
            res_copy(down, slot).start()

        @pl.when(place + slot >= slots)
        def _(up=up, slot=slot):
            res_copy(up, slot).start()

    for slot in range(slots):
        if not first:
            old_copy(slot).start()
    right = right_ref[...]
    left = left_ref[...]

    def forward(i, carry):
        z = i * STEP
        value = (res[pl.ds(z, STEP)] * src[pl.ds(z, STEP)]).reshape(STEP * n, n)
        value = table_times(left, beside(times_table(value, right), STEP))
        for k in range(STEP):
            work[pl.ds((z + k) * n, n), :] = value[:, k * n : (k + 1) * n]
        return carry

    for slab in range(slabs):
        if slab % 2 == 0:
            res_copy(res_refs[0], slab // 2).wait()
        src_copy(src_refs[0].at[0], slab).wait()
        lax.fori_loop(slab * slab_len // STEP, (slab + 1) * slab_len // STEP, forward, 0)

    scale = 4.0 * math.pi / float(n) ** 3

    def columns(i, carry):
        y = i * STEP
        value = jnp.concatenate([work[pl.ds(y + k, n, stride=n), :] for k in range(STEP)], 1)
        value = table_times(left, value)
        plane = gz_ref[...] + gx_ref[...] + KAPPA_SQ
        value = jnp.concatenate(
            [
                value[:, k * n : (k + 1) * n] * (scale / (plane + gz_ref[pl.ds(y + k, 1), :]))
                for k in range(STEP)
            ],
            1,
        )
        value = table_times(left, value)
        for k in range(STEP):
            work[pl.ds(y + k, n, stride=n), :] = value[:, k * n : (k + 1) * n]
        return carry

    lax.fori_loop(0, n // STEP, columns, 0)
    weight = -occ_ref[0]

    def backward(i, carry):
        z = i * STEP
        value = jnp.concatenate([work[pl.ds((z + k) * n, n), :] for k in range(STEP)], 1)
        value = times_table(below(table_times(left, value), STEP), right).reshape(STEP, n, n)
        value = value * (src[pl.ds(z, STEP)] * weight)
        if not first:
            value = value + acc[pl.ds(z, STEP)]
        acc[pl.ds(z, STEP)] = value
        return carry

    order = list(range(1, slots)) + [0]
    for slot in order:
        if not first:
            old_copy(slot).wait()
        lax.fori_loop(slot * slot_len // STEP, (slot + 1) * slot_len // STEP, backward, 0)
        out_copy(slot).start()
    for slot in order:
        out_copy(slot).wait()


def exchange(where, occ, res_pieces, src_pieces, old, tables, waves):
    right, left = tables
    slots = (len(res_pieces) + 1) // 2
    slot_len, n, _ = res_pieces[0].shape
    any_spec = pl.BlockSpec(memory_space=pl.ANY)
    vmem_spec = pl.BlockSpec(memory_space=pltpu.VMEM)
    smem_spec = pl.BlockSpec(memory_space=pltpu.SMEM)
    pieces = [*res_pieces, *src_pieces, *(old or [])]
    grid = pltpu.VMEM((n, n, n), F32)
    return pl.pallas_call(
        functools.partial(exchange_kernel, n, slots, old is None),
        out_shape=[jax.ShapeDtypeStruct((slot_len, n, n), F32)] * slots,
        in_specs=[smem_spec] * 2 + [vmem_spec] * 4 + [any_spec] * len(pieces),
        out_specs=[any_spec] * slots,
        scratch_shapes=[
            grid,
            grid,
            pltpu.VMEM((n * n, n), F32),
            grid,
            pltpu.SemaphoreType.DMA((slots,)),
            pltpu.SemaphoreType.DMA((2 * slots,)),
            pltpu.SemaphoreType.DMA((slots,)),
            pltpu.SemaphoreType.DMA((slots,)),
        ],
        compiler_params=pltpu.CompilerParams(vmem_limit_bytes=60 * 1024 * 1024),
        cost_estimate=pl.CostEstimate(flops=48 * n**4, bytes_accessed=16 * n**3, transcendentals=0),
        name="exchange",
    )(where, occ.reshape(1), waves[None, :], jnp.broadcast_to(waves[:, None], (n, n)), right, left, *pieces)


def whole_grids(resident, blocks, occupation):
    count_res, slab_len, n, _ = resident.shape
    slabs = lax.axis_size("slab")
    bands = lax.axis_size("band")
    planes = slabs // 2
    names = ("band", "slab")
    coords = [
        (x, c, z, y) for x in range(2) for c in range(2) for z in range(planes) for y in range(2)
    ]

    def flat(x, c, z, y):
        return ((x * 2 + c) * planes + z) * 2 + y

    def send(value, rule):
        pairs = []
        for coord in coords:
            target = rule(*coord)
            if target is not None:
                pairs.append((flat(*coord), flat(*target)))
        return lax.ppermute(value, names, pairs)

    band, slab = (lax.axis_index("band"), lax.axis_index("slab"))
    c, z, y = (band % 2, slab // 2, slab % 2)
    x = band // 2

    def swap_x(v):
        return send(v, lambda x, c, z, y: (1 - x, c, z, y))

    def swap_c(v):
        return send(v, lambda x, c, z, y: (x, 1 - c, z, y))

    def swap_y(v):
        return send(v, lambda x, c, z, y: (x, c, z, 1 - y))

    low = z < planes // 2
    first_half, last_half = (blocks[:2], blocks[2:])

    def to_low(x, c, z, y):
        return (x, z, 2 * c + x, y) if z < 2 else (1 - x, z - 2, 2 * c + x, y)

    def to_high(x, c, z, y):
        return (x, z - 2, 2 * c + x, y) if z >= 2 else (1 - x, z, 2 * c + x, y)

    part_1 = send(jnp.where(low, first_half, last_half), to_low)
    part_2 = send(jnp.where(low, last_half, first_half), to_high)
    own = [jnp.stack([part_1[k], part_2[k]]) for k in range(2)]

    straight = send(lax.dynamic_index_in_dim(resident, y, 0, False), lambda x, c, z, y: (x, y, z, c))
    crossed = send(lax.dynamic_index_in_dim(resident, 1 - y, 0, False), lambda x, c, z, y: (x, 1 - y, z, c))
    quarter = jnp.where(
        c == 0, jnp.concatenate([straight, crossed]), jnp.concatenate([crossed, straight])
    )
    downs, ups = ([], [])
    down = up = quarter
    for step in range(1, planes):
        down = send(down, lambda x, c, z, y: (x, c, z - 1, y) if 1 <= z <= planes - step else None)
        up = send(up, lambda x, c, z, y: (x, c, z + 1, y) if step - 1 <= z < planes - 1 else None)
        downs.append(down)
        ups.append(up)
    res_pieces = [quarter, *downs, *ups]

    beside_y = [swap_y(own[0]), swap_y(own[1])]
    beside_x = [swap_x(own[0]), swap_x(own[1])]
    corner = [swap_y(beside_x[0]), swap_x(beside_y[1])]
    pieces = [(own[0], beside_y[0]), (own[1], beside_y[1]), (beside_x[0], corner[0]), (beside_x[1], corner[1])]

    turned = (x + z) % 2
    quad = 2 * (z % 2) + z // 2
    tables = cas_tables(n)
    waves = wave_of(jnp.arange(n, dtype=jnp.int32), n) ** 2
    total = None
    for index, (same, other) in enumerate(pieces):
        flip = turned if index < 2 else 1 - turned
        where = []
        for core in (c, 1 - c):
            for parity in (y, 1 - y):
                for half in (flip, 1 - flip):
                    where.append((core + 2 * half + planes - z) % planes * 2 + parity)
        where = jnp.stack([*where, z]).astype(jnp.int32)
        occ = lax.dynamic_index_in_dim(occupation, 4 * quad + 2 * flip + index % 2, 0, False)
        total = exchange(where, occ, res_pieces, [same, other, swap_c(same), swap_c(other)], total, tables, waves)

    down = up = None
    for step in range(1, planes):
        low_part, high_part = (total[step], total[planes - step])
        if step > 1:
            low_part, high_part = (low_part + down, high_part + up)
        down = send(low_part, lambda x, c, z, y: (x, c, z - 1, y) if z >= planes - step and z >= 1 else None)
        up = send(high_part, lambda x, c, z, y: (x, c, z + 1, y) if z <= step - 1 and z < planes - 1 else None)
    summed = total[0] + down + up
    near, far = (summed[:slab_len], summed[slab_len:])
    back = send(jnp.where(c == 0, near, far), lambda x, c, z, y: (x, y, z, c))
    cross = send(jnp.where(c == 0, far, near), lambda x, c, z, y: (x, y, z, 1 - c))
    return jnp.where(y == 0, jnp.stack([back, cross]), jnp.stack([cross, back]))


def per_device(resident, blocks, occupation):
    if (
        lax.axis_size("band") == 4
        and lax.axis_size("slab") == 8
        and resident.shape[0] == 2
        and blocks.shape[0] == 4
        and resident.shape[1] % STEP == 0
    ):
        return whole_grids(resident, blocks, occupation)
    return sliced_grids(resident, blocks, occupation)


def solution(mesh):
    placed = (P("band", "slab", None, None), P("band", "slab", None, None), P())
    return jax.shard_map(
        per_device,
        mesh=mesh,
        in_specs=placed,
        out_specs=P("band", "slab", None, None),
        check_vma=False,
    )
```

```python
import functools
import math

import jax
import jax.numpy as jnp
from jax import lax
from jax.experimental import pallas as pl
from jax.experimental.pallas import tpu as pltpu
from jax.sharding import PartitionSpec as P

KAPPA_SQ = 0.01
F32, BF16 = (jnp.float32, jnp.bfloat16)


def dft_tables(grid_len):
    indices = jnp.arange(grid_len, dtype=jnp.int32)
    product = indices[:, None] * indices[None, :] % grid_len
    angles = product.astype(jnp.float32) * (2.0 * math.pi / grid_len)
    return (jnp.cos(angles), jnp.sin(angles))


def transform(real_part, imag_part, form, cos_t, sin_t, sign_val):

    def apply(values, table):
        return jnp.einsum(
            form, values, table, precision=lax.Precision.HIGHEST, preferred_element_type=jnp.float32
        )

    real_cos = apply(real_part, cos_t)
    real_sin = apply(real_part, sin_t)
    imag_cos = apply(imag_part, cos_t)
    imag_sin = apply(imag_part, sin_t)
    return (real_cos - sign_val * imag_sin, imag_cos + sign_val * real_sin)


def wave_of(indices, grid_len):
    signed = jnp.where(indices > (grid_len - 1) // 2, indices - grid_len, indices)
    return signed.astype(jnp.float32) * (2.0 * math.pi / grid_len)


def coulomb(wave_z, wave_y, wave_x):
    squared = wave_z[:, None, None] ** 2 + wave_y[None, :, None] ** 2 + wave_x[None, None, :] ** 2
    return 4.0 * math.pi / (squared + KAPPA_SQ)


def sliced_grids(resident, blocks, occupation):
    orb_count, plane_count, grid_len, _ = resident.shape
    local_src = blocks.shape[0]
    group_count = lax.axis_size("band")
    src_count = local_src * group_count
    cos_t, sin_t = dft_tables(grid_len)
    along_x = "fzyx,xk->fzyk"
    along_y = "fzyx,yk->fzkx"
    along_z = "fzyx,zk->fkyx"
    source = lax.all_gather(blocks, "band", axis=0, tiled=True)
    count_pairs = source.shape[0] // 2
    even_src = source[0::2]
    odd_src = source[1::2]
    real_part = (resident[:, None] * even_src[None]).reshape(
        orb_count * count_pairs, plane_count, grid_len, grid_len
    )
    imag_part = (resident[:, None] * odd_src[None]).reshape(
        orb_count * count_pairs, plane_count, grid_len, grid_len
    )
    real_part, imag_part = transform(real_part, imag_part, along_x, cos_t, sin_t, -1.0)
    real_part, imag_part = transform(real_part, imag_part, along_y, cos_t, sin_t, -1.0)
    shaped = (orb_count, count_pairs, plane_count, grid_len, grid_len)
    real_part, imag_part = (real_part.reshape(shaped), imag_part.reshape(shaped))
    field_count = orb_count * (src_count // 2)
    flat = (field_count, plane_count, grid_len, grid_len)
    real_part = real_part.reshape(flat)
    imag_part = imag_part.reshape(flat)
    all_waves = wave_of(jnp.arange(grid_len, dtype=jnp.int32), grid_len)
    position = lax.axis_index("slab")
    col_real = lax.all_to_all(real_part, "slab", split_axis=2, concat_axis=1, tiled=True)
    col_imag = lax.all_to_all(imag_part, "slab", split_axis=2, concat_axis=1, tiled=True)
    width_y = col_real.shape[2]
    local_waves = wave_of(position * width_y + jnp.arange(width_y, dtype=jnp.int32), grid_len)
    kernel = coulomb(all_waves, local_waves, all_waves)
    col_real, col_imag = transform(col_real, col_imag, along_z, cos_t, sin_t, -1.0)
    col_real = col_real * kernel[None]
    col_imag = col_imag * kernel[None]
    col_real, col_imag = transform(col_real, col_imag, along_z, cos_t, sin_t, 1.0)
    real_part = lax.all_to_all(col_real, "slab", split_axis=1, concat_axis=2, tiled=True)
    imag_part = lax.all_to_all(col_imag, "slab", split_axis=1, concat_axis=2, tiled=True)
    real_part, imag_part = transform(real_part, imag_part, along_y, cos_t, sin_t, 1.0)
    real_part, imag_part = transform(real_part, imag_part, along_x, cos_t, sin_t, 1.0)
    scale_inv = 1.0 / float(grid_len * grid_len * grid_len)
    shaped = (orb_count, src_count // 2, plane_count, grid_len, grid_len)
    pot_even = real_part.reshape(shaped) * scale_inv
    pot_odd = imag_part.reshape(shaped) * scale_inv
    weighted_even = source[0::2] * occupation[0::2][:, None, None, None]
    weighted_odd = source[1::2] * occupation[1::2][:, None, None, None]
    summed = jnp.sum(pot_even * weighted_even[None], axis=1) + jnp.sum(
        pot_odd * weighted_odd[None], axis=1
    )
    return -summed


def halves(value):
    top = value.astype(BF16)
    return (top, (value - top.astype(F32)).astype(BF16))


def cas_tables(grid_len):
    indices = jnp.arange(grid_len, dtype=jnp.int32)
    product = indices[:, None] * indices[None, :] % grid_len
    angles = product.astype(F32) * (2.0 * math.pi / grid_len)
    table = jnp.cos(angles) + jnp.sin(angles)
    top = lax.reduce_precision(table, 8, 7)
    high, low = (top.astype(BF16), (table - top).astype(BF16))
    zero = jnp.zeros_like(high)
    right = jnp.block([[high, low], [high, zero]])
    left = jnp.block([[high, high], [low, zero]])
    return (right, left)


def times_table(rows, right):
    grid_len = rows.shape[1]
    both = jnp.dot(jnp.concatenate(halves(rows), 1), right, preferred_element_type=F32)
    return both[:, :grid_len] + both[:, grid_len:]


def table_times(left, cols):
    grid_len = cols.shape[0]
    both = jnp.dot(left, jnp.concatenate(halves(cols), 0), preferred_element_type=F32)
    return both[:grid_len] + both[grid_len:]


def beside(rows, count):
    size = rows.shape[0] // count
    return jnp.concatenate([rows[k * size : (k + 1) * size] for k in range(count)], 1)


def below(cols, count):
    size = cols.shape[1] // count
    return jnp.concatenate([cols[:, k * size : (k + 1) * size] for k in range(count)], 0)


STEP = 16
PAD = 8
PARTS = 2


def exchange_kernel(grid_len, slots, layout, where_ref, occ_ref, gx_ref, gz_ref, right_ref, left_ref, *refs):
    refs = list(refs)
    n = grid_len
    slot_len = n // slots
    slab_len = slot_len // 2
    part_len = slab_len // PARTS
    res_refs = [[refs.pop(0) for _ in range(2 * slots - 1)] for _ in range(2)]
    src_refs = [[(refs.pop(0), *place) for place in places] for places in layout]
    out_refs = [[refs.pop(0) for _ in range(PARTS)] for _ in range(slots)]
    res, src, work, acc, res_sem, src_sem, out_sem = refs
    core, parity, plane = (where_ref[0], where_ref[1], where_ref[2])
    count = len(src_refs)

    def res_copy(ref, kind, slot):
        side = core if kind == 0 else 1 - core
        start = slot * slot_len + side * slab_len
        return pltpu.make_async_copy(ref, res.at[pl.ds(start, slab_len)], res_sem.at[kind, slot])

    def src_copy(ref, buffer, slot, kind, part):
        side = parity if kind == 0 else 1 - parity
        start = slot * slot_len + side * slab_len + part * part_len
        return pltpu.make_async_copy(
            ref, src.at[buffer, pl.ds(start, part_len)], src_sem.at[buffer, slot, kind, part]
        )

    def load_source(index):
        for ref, first_slot, slot_count, kind, part in src_refs[index]:
            for k in range(slot_count):
                src_copy(ref.at[k], index % 2, first_slot + k, kind, part).start()

    def out_copies(slot):
        copies = []
        for part in range(PARTS):
            for side in range(2):
                start = slot * slot_len + side * slab_len + part * part_len
                copies.append(
                    pltpu.make_async_copy(
                        acc.at[pl.ds(start, part_len)],
                        out_refs[slot][part].at[pl.ds(side * part_len, part_len)],
                        out_sem.at[slot, part, side],
                    )
                )
        return copies

    load_source(0)
    for kind in range(2):
        res_copy(res_refs[kind][0], kind, 0).start()
        for slot in range(1, slots):
            down, up = (res_refs[kind][slot], res_refs[kind][slots - 1 + slots - slot])

            @pl.when(plane + slot < slots)
            def _(down=down, kind=kind, slot=slot):
                res_copy(down, kind, slot).start()

            @pl.when(plane + slot >= slots)
            def _(up=up, kind=kind, slot=slot):
                res_copy(up, kind, slot).start()

    if count > 1:
        load_source(1)
    right = right_ref[...]
    left = left_ref[...]
    scale = 4.0 * math.pi / float(n) ** 3
    steps = slot_len // STEP

    for index in range(count):
        buffer = index % 2
        weight = -occ_ref[index]

        def forward(i, carry, index=index, buffer=buffer):
            slot = i // steps

            @pl.when(i % steps == 0)
            def _():
                for kind in range(2):
                    if index == 0:
                        res_copy(res_refs[0][0], kind, slot).wait()
                    for part in range(PARTS):
                        src_copy(src_refs[0][0][0].at[0], buffer, slot, kind, part).wait()

            z = i * STEP
            value = (res[pl.ds(z, STEP)] * src[buffer, pl.ds(z, STEP)]).reshape(STEP * n, n)
            value = table_times(left, beside(times_table(value, right), STEP))
            for k in range(STEP):
                work[pl.ds((z + k) * (n + PAD), n), :] = value[:, k * n : (k + 1) * n]
            return carry

        lax.fori_loop(0, n // STEP, forward, 0)

        def columns(i, carry):
            y = i * STEP
            value = jnp.concatenate(
                [work[pl.ds(y + k, n, stride=n + PAD), :] for k in range(STEP)], 1
            )
            value = table_times(left, value)
            base = gz_ref[...] + (gx_ref[...] + KAPPA_SQ)
            value = jnp.concatenate(
                [
                    value[:, k * n : (k + 1) * n] * (scale / (base + gz_ref[pl.ds(y + k, 1), :]))
                    for k in range(STEP)
                ],
                1,
            )
            value = table_times(left, value)
            for k in range(STEP):
                work[pl.ds(y + k, n, stride=n + PAD), :] = value[:, k * n : (k + 1) * n]
            return carry

        lax.fori_loop(0, n // STEP, columns, 0)

        def backward(i, carry, index=index, buffer=buffer, weight=weight):
            turn = i // steps
            slot = jnp.where(turn == slots - 1, 0, jnp.where(turn % 2 == 0, 1 + turn // 2, slots - 1 - turn // 2))
            z = (slot * steps + i % steps) * STEP
            value = jnp.concatenate([work[pl.ds((z + k) * (n + PAD), n), :] for k in range(STEP)], 1)
            value = times_table(below(table_times(left, value), STEP), right).reshape(STEP, n, n)
            value = value * (src[buffer, pl.ds(z, STEP)] * weight)
            if index > 0:
                value = value + acc[pl.ds(z, STEP)]
            acc[pl.ds(z, STEP)] = value
            if index == count - 1:
                for done in range(slots):

                    @pl.when((i % steps == steps - 1) & (slot == done))
                    def _(done=done):
                        for copy in out_copies(done):
                            copy.start()

            return carry

        lax.fori_loop(0, n // STEP, backward, 0)
        if index + 2 < count:
            load_source(index + 2)
    for slot in range(slots):
        for copy in out_copies(slot):
            copy.wait()


def exchange(where, occ, res_pieces, src_pieces, tables, waves):
    right, left = tables
    slots = (len(res_pieces[0]) + 1) // 2
    slab_len, n, _ = res_pieces[0][0].shape
    any_spec = pl.BlockSpec(memory_space=pl.ANY)
    vmem_spec = pl.BlockSpec(memory_space=pltpu.VMEM)
    smem_spec = pl.BlockSpec(memory_space=pltpu.SMEM)
    arrays = [*res_pieces[0], *res_pieces[1]]
    layout = []
    for pieces in src_pieces:
        layout.append([place for _, *place in pieces])
        arrays.extend(array for array, *_ in pieces)
    out = pl.pallas_call(
        functools.partial(exchange_kernel, n, slots, layout),
        out_shape=[jax.ShapeDtypeStruct((2 * slab_len // PARTS, n, n), F32)] * (slots * PARTS),
        in_specs=[smem_spec] * 2 + [vmem_spec] * 4 + [any_spec] * len(arrays),
        out_specs=[any_spec] * (slots * PARTS),
        scratch_shapes=[
            pltpu.VMEM((n, n, n), F32),
            pltpu.VMEM((2, n, n, n), F32),
            pltpu.VMEM((n * (n + PAD), n), F32),
            pltpu.VMEM((n, n, n), F32),
            pltpu.SemaphoreType.DMA((2, slots)),
            pltpu.SemaphoreType.DMA((2, slots, 2, PARTS)),
            pltpu.SemaphoreType.DMA((slots, PARTS, 2)),
        ],
        compiler_params=pltpu.CompilerParams(vmem_limit_bytes=56 * 2**20),
        cost_estimate=pl.CostEstimate(
            flops=48 * n**4 * len(layout), bytes_accessed=4 * n**3 * (2 + len(layout)), transcendentals=0
        ),
        name="exchange",
    )(where, occ, waves[None, :], jnp.broadcast_to(waves[:, None], (n, n)), right, left, *arrays)
    return [out[slot * PARTS : (slot + 1) * PARTS] for slot in range(slots)]


def whole_grids(resident, blocks, occupation):
    count_res, slab_len, n, _ = resident.shape
    planes = lax.axis_size("slab") // 2
    names = ("band", "slab")
    coords = [
        (x, c, z, y) for x in range(2) for c in range(2) for z in range(planes) for y in range(2)
    ]

    def flat(x, c, z, y):
        return ((x * 2 + c) * planes + z) * 2 + y

    def send(value, rule):
        pairs = []
        for coord in coords:
            target = rule(*coord)
            if target is not None:
                pairs.append((flat(*coord), flat(*target)))
        return lax.ppermute(value, names, pairs)

    band, slab = (lax.axis_index("band"), lax.axis_index("slab"))
    c, z, y = (band % 2, slab // 2, slab % 2)
    x = band // 2

    def swap_x(v):
        return send(v, lambda x, c, z, y: (1 - x, c, z, y))

    def swap_c(v):
        return send(v, lambda x, c, z, y: (x, 1 - c, z, y))

    def swap_y(v):
        return send(v, lambda x, c, z, y: (x, c, z, 1 - y))

    def pick(values, index):
        out = values[0]
        for k in range(1, len(values)):
            out = jnp.where(index == k, values[k], out)
        return out

    part_len = slab_len // PARTS
    own = []
    for part in range(PARTS):
        rows = slice(part * part_len, (part + 1) * part_len)
        quads = [lax.dynamic_index_in_dim(blocks, band, 0, False)[rows]]
        for other in range(1, 4):
            dx, dc = (other // 2, other % 2)
            value = lax.dynamic_index_in_dim(blocks, band ^ other, 0, False)[rows]
            quads.append(send(value, lambda x, c, z, y, dx=dx, dc=dc: (x ^ dx, c ^ dc, z, y)))
        slots = [pick(quads, z ^ band)]
        for step in range(1, planes):
            value = pick(quads, ((z + step) % planes) ^ band)
            slots.append(send(value, lambda x, c, z, y, step=step: (x, c, (z + step) % planes, y)))
        own.append(jnp.stack([slots[0], *slots[:0:-1]]))

    res_pieces = []
    for kind in range(2):
        piece = lax.dynamic_index_in_dim(resident, y if kind == 0 else 1 - y, 0, False)
        piece = send(piece, lambda x, c, z, y, kind=kind: (x, y ^ kind, z, c))
        downs, ups = ([], [])
        down = up = piece
        for step in range(1, planes):
            down = send(down, lambda x, c, z, y: (x, c, z - 1, y) if 1 <= z <= planes - step else None)
            up = send(up, lambda x, c, z, y: (x, c, z + 1, y) if step - 1 <= z < planes - 1 else None)
            downs.append(down)
            ups.append(up)
        res_pieces.append([piece, *downs, *ups])

    near, far = ([], [])
    half = planes // 2
    for part in range(PARTS):
        beside_y = swap_y(own[part])
        beside_x = swap_x(own[part])
        low = swap_y(beside_x[:half])
        high = swap_x(beside_y[half:])
        near += [(own[part], 0, planes, 0, part), (beside_y, 0, planes, 1, part)]
        far += [
            (beside_x, 0, planes, 0, part),
            (low, 0, half, 1, part),
            (high, half, half, 1, part),
        ]

    def swapped(pieces):
        return [(swap_c(array), *place) for array, *place in pieces]

    sources = [near, swapped(near), far, swapped(far)]
    occ = jnp.stack(
        [
            lax.dynamic_index_in_dim(occupation, 4 * z + (band ^ other), 0, False)
            for other in (0, 1, 2, 3)
        ]
    )
    where = jnp.stack([c, y, z]).astype(jnp.int32)
    waves = wave_of(jnp.arange(n, dtype=jnp.int32), n) ** 2
    total = exchange(where, occ, res_pieces, sources, cas_tables(n), waves)

    rows = []
    for part in range(PARTS):
        down = up = None
        for step in range(1, planes):
            low, high = (total[step][part], total[planes - step][part])
            if step > 1:
                low, high = (low + down, high + up)
            down = send(low, lambda x, c, z, y: (x, c, z - 1, y) if z >= max(planes - step, 1) else None)
            up = send(high, lambda x, c, z, y: (x, c, z + 1, y) if z <= min(step - 1, planes - 2) else None)
        summed = total[0][part] + down + up
        first, last = (summed[:part_len], summed[part_len:])
        back = send(jnp.where(c == 0, first, last), lambda x, c, z, y: (x, y, z, c))
        cross = send(jnp.where(c == 0, last, first), lambda x, c, z, y: (x, y, z, 1 - c))
        rows.append(jnp.where(y == 0, jnp.stack([back, cross]), jnp.stack([cross, back])))
    return jnp.concatenate(rows, 1)


def per_device(resident, blocks, occupation):
    if (
        lax.axis_size("band") == 4
        and lax.axis_size("slab") == 8
        and resident.shape[0] == 2
        and blocks.shape[0] == 4
        and resident.shape[1] % STEP == 0
    ):
        return whole_grids(resident, blocks, occupation)
    return sliced_grids(resident, blocks, occupation)


def solution(mesh):
    placed = (P("band", "slab", None, None), P("band", "slab", None, None), P())
    return jax.shard_map(
        per_device,
        mesh=mesh,
        in_specs=placed,
        out_specs=P("band", "slab", None, None),
        check_vma=False,
    )
```

```python
import functools
import math

import jax
import jax.numpy as jnp
from jax import lax
from jax.experimental import pallas as pl
from jax.experimental.pallas import tpu as pltpu
from jax.sharding import PartitionSpec as P


KAPPA_SQ = 0.01
F32, BF16 = (jnp.float32, jnp.bfloat16)


def dft_tables(grid_len):
    indices = jnp.arange(grid_len, dtype=jnp.int32)
    product = indices[:, None] * indices[None, :] % grid_len
    angles = product.astype(jnp.float32) * (2.0 * math.pi / grid_len)
    return (jnp.cos(angles), jnp.sin(angles))


def transform(real_part, imag_part, form, cos_t, sin_t, sign_val):

    def apply(values, table):
        return jnp.einsum(
            form, values, table, precision=lax.Precision.HIGHEST, preferred_element_type=jnp.float32
        )

    real_cos = apply(real_part, cos_t)
    real_sin = apply(real_part, sin_t)
    imag_cos = apply(imag_part, cos_t)
    imag_sin = apply(imag_part, sin_t)
    return (real_cos - sign_val * imag_sin, imag_cos + sign_val * real_sin)


def wave_of(indices, grid_len):
    signed = jnp.where(indices > (grid_len - 1) // 2, indices - grid_len, indices)
    return signed.astype(jnp.float32) * (2.0 * math.pi / grid_len)


def coulomb(wave_z, wave_y, wave_x):
    squared = wave_z[:, None, None] ** 2 + wave_y[None, :, None] ** 2 + wave_x[None, None, :] ** 2
    return 4.0 * math.pi / (squared + KAPPA_SQ)


def sliced_grids(resident, blocks, occupation):
    orb_count, plane_count, grid_len, _ = resident.shape
    local_src = blocks.shape[0]
    group_count = lax.axis_size("band")
    src_count = local_src * group_count
    cos_t, sin_t = dft_tables(grid_len)
    along_x = "fzyx,xk->fzyk"
    along_y = "fzyx,yk->fzkx"
    along_z = "fzyx,zk->fkyx"
    source = lax.all_gather(blocks, "band", axis=0, tiled=True)
    count_pairs = source.shape[0] // 2
    even_src = source[0::2]
    odd_src = source[1::2]
    real_part = (resident[:, None] * even_src[None]).reshape(
        orb_count * count_pairs, plane_count, grid_len, grid_len
    )
    imag_part = (resident[:, None] * odd_src[None]).reshape(
        orb_count * count_pairs, plane_count, grid_len, grid_len
    )
    real_part, imag_part = transform(real_part, imag_part, along_x, cos_t, sin_t, -1.0)
    real_part, imag_part = transform(real_part, imag_part, along_y, cos_t, sin_t, -1.0)
    shaped = (orb_count, count_pairs, plane_count, grid_len, grid_len)
    real_part, imag_part = (real_part.reshape(shaped), imag_part.reshape(shaped))
    field_count = orb_count * (src_count // 2)
    flat = (field_count, plane_count, grid_len, grid_len)
    real_part = real_part.reshape(flat)
    imag_part = imag_part.reshape(flat)
    all_waves = wave_of(jnp.arange(grid_len, dtype=jnp.int32), grid_len)
    position = lax.axis_index("slab")
    col_real = lax.all_to_all(real_part, "slab", split_axis=2, concat_axis=1, tiled=True)
    col_imag = lax.all_to_all(imag_part, "slab", split_axis=2, concat_axis=1, tiled=True)
    width_y = col_real.shape[2]
    local_waves = wave_of(position * width_y + jnp.arange(width_y, dtype=jnp.int32), grid_len)
    kernel = coulomb(all_waves, local_waves, all_waves)
    col_real, col_imag = transform(col_real, col_imag, along_z, cos_t, sin_t, -1.0)
    col_real = col_real * kernel[None]
    col_imag = col_imag * kernel[None]
    col_real, col_imag = transform(col_real, col_imag, along_z, cos_t, sin_t, 1.0)
    real_part = lax.all_to_all(col_real, "slab", split_axis=1, concat_axis=2, tiled=True)
    imag_part = lax.all_to_all(col_imag, "slab", split_axis=1, concat_axis=2, tiled=True)
    real_part, imag_part = transform(real_part, imag_part, along_y, cos_t, sin_t, 1.0)
    real_part, imag_part = transform(real_part, imag_part, along_x, cos_t, sin_t, 1.0)
    scale_inv = 1.0 / float(grid_len * grid_len * grid_len)
    shaped = (orb_count, src_count // 2, plane_count, grid_len, grid_len)
    pot_even = real_part.reshape(shaped) * scale_inv
    pot_odd = imag_part.reshape(shaped) * scale_inv
    weighted_even = source[0::2] * occupation[0::2][:, None, None, None]
    weighted_odd = source[1::2] * occupation[1::2][:, None, None, None]
    summed = jnp.sum(pot_even * weighted_even[None], axis=1) + jnp.sum(
        pot_odd * weighted_odd[None], axis=1
    )
    return -summed


def halves(value):
    top = value.astype(BF16)
    return (top, (value - top.astype(F32)).astype(BF16))


def cas_tables(grid_len):
    indices = jnp.arange(grid_len, dtype=jnp.int32)
    product = indices[:, None] * indices[None, :] % grid_len
    angles = product.astype(F32) * (2.0 * math.pi / grid_len)
    table = jnp.cos(angles) + jnp.sin(angles)
    top = lax.reduce_precision(table, 8, 7)
    high, low = (top.astype(BF16), (table - top).astype(BF16))
    zero = jnp.zeros_like(high)
    right = jnp.block([[high, low], [high, zero]])
    left = jnp.block([[high, high], [low, zero]])
    return (right, left)


def times_table(rows, right):
    grid_len = rows.shape[1]
    both = jnp.dot(jnp.concatenate(halves(rows), 1), right, preferred_element_type=F32)
    return both[:, :grid_len] + both[:, grid_len:]


def table_times(left, cols):
    grid_len = cols.shape[0]
    both = jnp.dot(left, jnp.concatenate(halves(cols), 0), preferred_element_type=F32)
    return both[:grid_len] + both[grid_len:]


def beside(rows, count):
    size = rows.shape[0] // count
    return jnp.concatenate([rows[k * size : (k + 1) * size] for k in range(count)], 1)


def below(cols, count):
    size = cols.shape[1] // count
    return jnp.concatenate([cols[:, k * size : (k + 1) * size] for k in range(count)], 0)


STEP = 16
PAD = 8
PARTS = 2


def exchange_kernel(grid_len, slots, layout, last, where_ref, occ_ref, gx_ref, gz_ref, right_ref, left_ref, *refs):
    refs = list(refs)
    n = grid_len
    slot_len = n // slots
    slab_len = slot_len // 2
    part_len = slab_len // PARTS
    res_refs = [[refs.pop(0) for _ in range(slots)] for _ in range(2)]
    src_refs = [(refs.pop(0), *place) for place in layout]
    old_ref = refs.pop(0) if last else None
    out_refs = [refs.pop(0) for _ in range(3 if last else 1)]
    res, src, work, acc, res_sem, src_sem, old_sem, out_sem = refs
    core, parity = (where_ref[0], where_ref[1])

    def res_copy(ref, kind, slot):
        side = core if kind == 0 else 1 - core
        start = slot * slot_len + side * slab_len
        return pltpu.make_async_copy(ref, res.at[pl.ds(start, slab_len)], res_sem.at[kind, slot])

    def src_copy(ref, slot, kind, part):
        side = parity if kind == 0 else 1 - parity
        start = slot * slot_len + side * slab_len + part * part_len
        return pltpu.make_async_copy(ref, src.at[pl.ds(start, part_len)], src_sem.at[slot, kind, part])

    def old_copy(slot):
        span = pl.ds(slot * slot_len, slot_len)
        return pltpu.make_async_copy(old_ref.at[span], acc.at[span], old_sem.at[slot])

    def out_copies(slot):
        if not last:
            span = pl.ds(slot * slot_len, slot_len)
            return [pltpu.make_async_copy(acc.at[span], out_refs[0].at[span], out_sem.at[slot, 0])]
        keep = acc.at[pl.ds(slot * slot_len + core * slab_len, slab_len)]
        give = acc.at[pl.ds(slot * slot_len + (1 - core) * slab_len, slab_len)]
        target = out_refs[1 if slot % 2 == 1 else 2].at[slot // 2]
        return [
            pltpu.make_async_copy(keep, out_refs[0].at[slot], out_sem.at[slot, 0]),
            pltpu.make_async_copy(give, target, out_sem.at[slot, 1]),
        ]

    for slot in range(slots):
        for kind in range(2):
            res_copy(res_refs[kind][slot], kind, slot).start()
        for ref, first_slot, slot_count, kind, part in src_refs:
            if first_slot <= slot < first_slot + slot_count:
                src_copy(ref.at[slot - first_slot], slot, kind, part).start()
    if last:
        for slot in range(slots):
            old_copy(slot).start()
    right = right_ref[...]
    left = left_ref[...]
    scale = 4.0 * math.pi / float(n) ** 3
    steps = slot_len // STEP
    weight = -occ_ref[0]

    def forward(i, carry):
        slot = i // steps

        @pl.when(i % steps == 0)
        def _():
            for kind in range(2):
                res_copy(res_refs[0][0], kind, slot).wait()
                for part in range(PARTS):
                    src_copy(src_refs[0][0].at[0], slot, kind, part).wait()

        z = i * STEP
        value = (res[pl.ds(z, STEP)] * src[pl.ds(z, STEP)]).reshape(STEP * n, n)
        value = table_times(left, beside(times_table(value, right), STEP))
        for k in range(STEP):
            work[pl.ds((z + k) * (n + PAD), n), :] = value[:, k * n : (k + 1) * n]
        return carry

    lax.fori_loop(0, n // STEP, forward, 0)

    def columns(i, carry):
        y = i * STEP
        value = jnp.concatenate([work[pl.ds(y + k, n, stride=n + PAD), :] for k in range(STEP)], 1)
        value = table_times(left, value)
        base = gz_ref[...] + (gx_ref[...] + KAPPA_SQ)
        value = jnp.concatenate(
            [
                value[:, k * n : (k + 1) * n] * (scale / (base + gz_ref[pl.ds(y + k, 1), :]))
                for k in range(STEP)
            ],
            1,
        )
        value = table_times(left, value)
        for k in range(STEP):
            work[pl.ds(y + k, n, stride=n + PAD), :] = value[:, k * n : (k + 1) * n]
        return carry

    lax.fori_loop(0, n // STEP, columns, 0)

    def backward(i, carry):
        turn = i // steps
        half = slots // 2
        slot = jnp.where(turn < half, 2 * turn + 1, 2 * (turn - half))
        if last:

            @pl.when(i % steps == 0)
            def _():
                old_copy(slot).wait()

        z = (slot * steps + i % steps) * STEP
        value = jnp.concatenate([work[pl.ds((z + k) * (n + PAD), n), :] for k in range(STEP)], 1)
        value = times_table(below(table_times(left, value), STEP), right).reshape(STEP, n, n)
        value = value * (src[pl.ds(z, STEP)] * weight)
        if last:
            value = value + acc[pl.ds(z, STEP)]
        acc[pl.ds(z, STEP)] = value
        for done in range(slots):

            @pl.when((i % steps == steps - 1) & (slot == done))
            def _(done=done):
                for copy in out_copies(done):
                    copy.start()

        return carry

    lax.fori_loop(0, n // STEP, backward, 0)
    for slot in range(slots):
        for copy in out_copies(slot):
            copy.wait()


def exchange(where, occ, res_pieces, src_pieces, old, tables, waves):
    right, left = tables
    slots = len(res_pieces[0])
    slab_len, n, _ = res_pieces[0][0].shape
    last = old is not None
    any_spec = pl.BlockSpec(memory_space=pl.ANY)
    vmem_spec = pl.BlockSpec(memory_space=pltpu.VMEM)
    smem_spec = pl.BlockSpec(memory_space=pltpu.SMEM)
    layout = [place for _, *place in src_pieces]
    arrays = [*res_pieces[0], *res_pieces[1], *[array for array, *_ in src_pieces]]
    if last:
        arrays.append(old)
        shapes = [(slots, slab_len, n, n), (slots // 2, slab_len, n, n), (slots // 2, slab_len, n, n)]
    else:
        shapes = [(n, n, n)]
    return pl.pallas_call(
        functools.partial(exchange_kernel, n, slots, layout, last),
        out_shape=[jax.ShapeDtypeStruct(shape, F32) for shape in shapes],
        in_specs=[smem_spec] * 2 + [vmem_spec] * 4 + [any_spec] * len(arrays),
        out_specs=[any_spec] * len(shapes),
        scratch_shapes=[
            pltpu.VMEM((n, n, n), F32),
            pltpu.VMEM((n, n, n), F32),
            pltpu.VMEM((n * (n + PAD), n), F32),
            pltpu.VMEM((n, n, n), F32),
            pltpu.SemaphoreType.DMA((2, slots)),
            pltpu.SemaphoreType.DMA((slots, 2, PARTS)),
            pltpu.SemaphoreType.DMA((slots,)),
            pltpu.SemaphoreType.DMA((slots, 2)),
        ],
        compiler_params=pltpu.CompilerParams(vmem_limit_bytes=48 * 2**20),
        cost_estimate=pl.CostEstimate(
            flops=72 * n**4, bytes_accessed=4 * n**3 * (5 if last else 3), transcendentals=0
        ),
        name="exchange",
    )(where, occ.reshape(1), waves[None, :], jnp.broadcast_to(waves[:, None], (n, n)), right, left, *arrays)


def whole_grids(resident, blocks, occupation):
    count_res, slab_len, n, _ = resident.shape
    planes = lax.axis_size("slab") // 2
    names = ("band", "slab")
    coords = [
        (x, c, z, y) for x in range(2) for c in range(2) for z in range(planes) for y in range(2)
    ]

    def flat(x, c, z, y):
        return ((x * 2 + c) * planes + z) * 2 + y

    def send(value, rule):
        pairs = []
        for coord in coords:
            target = rule(*coord)
            if target is not None:
                pairs.append((flat(*coord), flat(*target)))
        return lax.ppermute(value, names, pairs)

    band, slab = (lax.axis_index("band"), lax.axis_index("slab"))
    c, z, y = (band % 2, slab // 2, slab % 2)

    def swap_x(v):
        return send(v, lambda x, c, z, y: (1 - x, c, z, y))

    def swap_c(v):
        return send(v, lambda x, c, z, y: (x, 1 - c, z, y))

    def swap_y(v):
        return send(v, lambda x, c, z, y: (x, c, z, 1 - y))

    def turn_cy(v):
        return send(v, lambda x, c, z, y: (x, y, z, c))

    def pick(values, index):
        out = values[0]
        for k in range(1, len(values)):
            out = jnp.where(index == k, values[k], out)
        return out

    part_len = slab_len // PARTS
    own = []
    for part in range(PARTS):
        rows = slice(part * part_len, (part + 1) * part_len)
        quads = [lax.dynamic_index_in_dim(blocks, band, 0, False)[rows]]
        for other in range(1, 4):
            dx, dc = (other // 2, other % 2)
            value = lax.dynamic_index_in_dim(blocks, band ^ other, 0, False)[rows]
            quads.append(send(value, lambda x, c, z, y, dx=dx, dc=dc: (x ^ dx, c ^ dc, z, y)))
        slots = [pick(quads, z ^ band)]
        for step in range(1, planes):
            value = pick(quads, ((z + step) % planes) ^ band)
            slots.append(send(value, lambda x, c, z, y, step=step: (x, c, (z + step) % planes, y)))
        own.append(jnp.stack([slots[0], *slots[:0:-1]]))

    residents = []
    for r in range(count_res):
        piece = turn_cy(resident[r])
        downs, ups = ([], [])
        down = up = piece
        for step in range(1, planes):
            if r == 0 and step == 2:
                down, up, _ = lax.optimization_barrier((down, up, own[-1]))
            if r > 0 and step == 1:
                down, up, earlier = lax.optimization_barrier((down, up, earlier))
            down = send(down, lambda x, c, z, y: (x, c, z - 1, y) if 1 <= z <= planes - step else None)
            up = send(up, lambda x, c, z, y: (x, c, z + 1, y) if step - 1 <= z < planes - 1 else None)
            downs.append(down)
            ups.append(up)
        earlier = downs[1]
        slots = [piece]
        for step in range(1, planes):
            slots.append(jnp.where(z + step < planes, downs[step - 1], ups[planes - step - 1]))
        residents.append([slots, [swap_c(v) for v in slots]])

    near, far = ([], [])
    half = planes // 2
    for part in range(PARTS):
        beside_y = swap_y(own[part])
        beside_x = swap_x(own[part])
        low = swap_y(beside_x[:half])
        high = swap_x(beside_y[half:])
        near += [(own[part], 0, planes, 0, part), (beside_y, 0, planes, 1, part)]
        far += [
            (beside_x, 0, planes, 0, part),
            (low, 0, half, 1, part),
            (high, half, half, 1, part),
        ]

    occ = [lax.dynamic_index_in_dim(occupation, 4 * z + (band ^ other), 0, False) for other in (0, 2)]
    where = jnp.stack([c, y]).astype(jnp.int32)
    waves = wave_of(jnp.arange(n, dtype=jnp.int32), n) ** 2
    tables = cas_tables(n)
    rows, ties = ([], [where, where])
    for r in range(count_res):
        (old,) = exchange(ties[0], occ[0], residents[r], near, None, tables, waves)
        keep, odd, even = exchange(ties[1], occ[1], residents[r], far, old, tables, waves)
        odd, even = (swap_c(odd), swap_c(even))

        terms = {}
        for part, array in ((1, odd), (0, even)):
            slots = range(part, planes, 2)
            sums = [keep[slot] + array[slot // 2] for slot in slots]
            terms.update(zip(slots, lax.optimization_barrier(sums)))

        down = up = None
        for step in range(1, planes):
            low, high = (terms[step], terms[planes - step])
            if step > 1:
                low, high = (low + down, high + up)
            if r + 1 < count_res and step < planes - 1:
                low, high, ties[step - 1] = lax.optimization_barrier((low, high, where))
            down = send(low, lambda x, c, z, y: (x, c, z - 1, y) if z >= max(planes - step, 1) else None)
            up = send(high, lambda x, c, z, y: (x, c, z + 1, y) if z <= min(step - 1, planes - 2) else None)
        rows.append(turn_cy(terms[0] + down + up))
    return jnp.stack(rows)


def per_device(resident, blocks, occupation):
    if (
        lax.axis_size("band") == 4
        and lax.axis_size("slab") == 8
        and resident.shape[0] == 2
        and blocks.shape[0] == 4
        and resident.shape[1] % STEP == 0
    ):
        return whole_grids(resident, blocks, occupation)
    return sliced_grids(resident, blocks, occupation)


def solution(mesh):
    placed = (P("band", "slab", None, None), P("band", "slab", None, None), P())
    return jax.shard_map(
        per_device,
        mesh=mesh,
        in_specs=placed,
        out_specs=P("band", "slab", None, None),
        check_vma=False,
    )
```

```python
import functools
import math

import jax
import jax.numpy as jnp
from jax import lax
from jax.experimental import pallas as pl
from jax.experimental.pallas import tpu as pltpu
from jax.sharding import PartitionSpec as P


KAPPA_SQ = 0.01
F32, BF16 = (jnp.float32, jnp.bfloat16)


def dft_tables(grid_len):
    indices = jnp.arange(grid_len, dtype=jnp.int32)
    product = indices[:, None] * indices[None, :] % grid_len
    angles = product.astype(jnp.float32) * (2.0 * math.pi / grid_len)
    return (jnp.cos(angles), jnp.sin(angles))


def transform(real_part, imag_part, form, cos_t, sin_t, sign_val):

    def apply(values, table):
        return jnp.einsum(
            form, values, table, precision=lax.Precision.HIGHEST, preferred_element_type=jnp.float32
        )

    real_cos = apply(real_part, cos_t)
    real_sin = apply(real_part, sin_t)
    imag_cos = apply(imag_part, cos_t)
    imag_sin = apply(imag_part, sin_t)
    return (real_cos - sign_val * imag_sin, imag_cos + sign_val * real_sin)


def wave_of(indices, grid_len):
    signed = jnp.where(indices > (grid_len - 1) // 2, indices - grid_len, indices)
    return signed.astype(jnp.float32) * (2.0 * math.pi / grid_len)


def coulomb(wave_z, wave_y, wave_x):
    squared = wave_z[:, None, None] ** 2 + wave_y[None, :, None] ** 2 + wave_x[None, None, :] ** 2
    return 4.0 * math.pi / (squared + KAPPA_SQ)


def sliced_grids(resident, blocks, occupation):
    orb_count, plane_count, grid_len, _ = resident.shape
    local_src = blocks.shape[0]
    group_count = lax.axis_size("band")
    src_count = local_src * group_count
    cos_t, sin_t = dft_tables(grid_len)
    along_x = "fzyx,xk->fzyk"
    along_y = "fzyx,yk->fzkx"
    along_z = "fzyx,zk->fkyx"
    source = lax.all_gather(blocks, "band", axis=0, tiled=True)
    count_pairs = source.shape[0] // 2
    even_src = source[0::2]
    odd_src = source[1::2]
    real_part = (resident[:, None] * even_src[None]).reshape(
        orb_count * count_pairs, plane_count, grid_len, grid_len
    )
    imag_part = (resident[:, None] * odd_src[None]).reshape(
        orb_count * count_pairs, plane_count, grid_len, grid_len
    )
    real_part, imag_part = transform(real_part, imag_part, along_x, cos_t, sin_t, -1.0)
    real_part, imag_part = transform(real_part, imag_part, along_y, cos_t, sin_t, -1.0)
    shaped = (orb_count, count_pairs, plane_count, grid_len, grid_len)
    real_part, imag_part = (real_part.reshape(shaped), imag_part.reshape(shaped))
    field_count = orb_count * (src_count // 2)
    flat = (field_count, plane_count, grid_len, grid_len)
    real_part = real_part.reshape(flat)
    imag_part = imag_part.reshape(flat)
    all_waves = wave_of(jnp.arange(grid_len, dtype=jnp.int32), grid_len)
    position = lax.axis_index("slab")
    col_real = lax.all_to_all(real_part, "slab", split_axis=2, concat_axis=1, tiled=True)
    col_imag = lax.all_to_all(imag_part, "slab", split_axis=2, concat_axis=1, tiled=True)
    width_y = col_real.shape[2]
    local_waves = wave_of(position * width_y + jnp.arange(width_y, dtype=jnp.int32), grid_len)
    kernel = coulomb(all_waves, local_waves, all_waves)
    col_real, col_imag = transform(col_real, col_imag, along_z, cos_t, sin_t, -1.0)
    col_real = col_real * kernel[None]
    col_imag = col_imag * kernel[None]
    col_real, col_imag = transform(col_real, col_imag, along_z, cos_t, sin_t, 1.0)
    real_part = lax.all_to_all(col_real, "slab", split_axis=1, concat_axis=2, tiled=True)
    imag_part = lax.all_to_all(col_imag, "slab", split_axis=1, concat_axis=2, tiled=True)
    real_part, imag_part = transform(real_part, imag_part, along_y, cos_t, sin_t, 1.0)
    real_part, imag_part = transform(real_part, imag_part, along_x, cos_t, sin_t, 1.0)
    scale_inv = 1.0 / float(grid_len * grid_len * grid_len)
    shaped = (orb_count, src_count // 2, plane_count, grid_len, grid_len)
    pot_even = real_part.reshape(shaped) * scale_inv
    pot_odd = imag_part.reshape(shaped) * scale_inv
    weighted_even = source[0::2] * occupation[0::2][:, None, None, None]
    weighted_odd = source[1::2] * occupation[1::2][:, None, None, None]
    summed = jnp.sum(pot_even * weighted_even[None], axis=1) + jnp.sum(
        pot_odd * weighted_odd[None], axis=1
    )
    return -summed


def halves(value):
    top = value.astype(BF16)
    return (top, (value - top.astype(F32)).astype(BF16))


def cas_tables(grid_len):
    indices = jnp.arange(grid_len, dtype=jnp.int32)
    product = indices[:, None] * indices[None, :] % grid_len
    angles = product.astype(F32) * (2.0 * math.pi / grid_len)
    table = jnp.cos(angles) + jnp.sin(angles)
    top = lax.reduce_precision(table, 8, 7)
    high, low = (top.astype(BF16), (table - top).astype(BF16))
    zero = jnp.zeros_like(high)
    right = jnp.block([[high, low], [high, zero]])
    left = jnp.block([[high, high], [low, zero]])
    return (right, left)


def times_table(rows, right):
    grid_len = rows.shape[1]
    both = jnp.dot(jnp.concatenate(halves(rows), 1), right, preferred_element_type=F32)
    return both[:, :grid_len] + both[:, grid_len:]


def table_times(left, cols):
    grid_len = cols.shape[0]
    both = jnp.dot(left, jnp.concatenate(halves(cols), 0), preferred_element_type=F32)
    return both[:grid_len] + both[grid_len:]


def beside(rows, count):
    size = rows.shape[0] // count
    return jnp.concatenate([rows[k * size : (k + 1) * size] for k in range(count)], 1)


def below(cols, count):
    size = cols.shape[1] // count
    return jnp.concatenate([cols[:, k * size : (k + 1) * size] for k in range(count)], 0)


STEP = 32
PAD = 8
PARTS = 2


def exchange_kernel(grid_len, slots, layout, last, where_ref, occ_ref, gx_ref, gz_ref, right_ref, left_ref, *refs):
    refs = list(refs)
    n = grid_len
    slot_len = n // slots
    slab_len = slot_len // 2
    part_len = slab_len // PARTS
    res_refs = [[refs.pop(0) for _ in range(slots)] for _ in range(2)]
    src_refs = [(refs.pop(0), *place) for place in layout]
    old_ref = refs.pop(0) if last else None
    out_refs = [refs.pop(0) for _ in range(3 if last else 1)]
    res, src, work, acc, res_sem, src_sem, old_sem, out_sem = refs
    core, parity = (where_ref[0], where_ref[1])

    def res_copy(ref, kind, slot):
        side = core if kind == 0 else 1 - core
        start = slot * slot_len + side * slab_len
        return pltpu.make_async_copy(ref, res.at[pl.ds(start, slab_len)], res_sem.at[kind, slot])

    def src_copy(ref, slot, kind, part):
        side = parity if kind == 0 else 1 - parity
        start = slot * slot_len + side * slab_len + part * part_len
        return pltpu.make_async_copy(ref, src.at[pl.ds(start, part_len)], src_sem.at[slot, kind, part])

    def old_copy(slot):
        span = pl.ds(slot * slot_len, slot_len)
        return pltpu.make_async_copy(old_ref.at[span], acc.at[span], old_sem.at[slot])

    def out_copies(slot):
        if not last:
            span = pl.ds(slot * slot_len, slot_len)
            return [pltpu.make_async_copy(acc.at[span], out_refs[0].at[span], out_sem.at[slot, 0])]
        keep = acc.at[pl.ds(slot * slot_len + core * slab_len, slab_len)]
        give = acc.at[pl.ds(slot * slot_len + (1 - core) * slab_len, slab_len)]
        target = out_refs[1 if slot % 2 == 1 else 2].at[slot // 2]
        return [
            pltpu.make_async_copy(keep, out_refs[0].at[slot], out_sem.at[slot, 0]),
            pltpu.make_async_copy(give, target, out_sem.at[slot, 1]),
        ]

    for slot in range(slots):
        for kind in range(2):
            res_copy(res_refs[kind][slot], kind, slot).start()
        for ref, first_slot, slot_count, kind, part in src_refs:
            if first_slot <= slot < first_slot + slot_count:
                src_copy(ref.at[slot - first_slot], slot, kind, part).start()
    if last:
        for slot in range(slots):
            old_copy(slot).start()
    right = right_ref[...]
    left = left_ref[...]
    scale = 4.0 * math.pi / float(n) ** 3
    steps = slot_len // STEP
    weight = -occ_ref[0]

    def forward(i, carry):
        slot = i // steps

        @pl.when(i % steps == 0)
        def _():
            for kind in range(2):
                res_copy(res_refs[0][0], kind, slot).wait()
                for part in range(PARTS):
                    src_copy(src_refs[0][0].at[0], slot, kind, part).wait()

        z = i * STEP
        value = (res[pl.ds(z, STEP)] * src[pl.ds(z, STEP)]).reshape(STEP * n, n)
        value = table_times(left, beside(times_table(value, right), STEP))
        for k in range(STEP):
            work[pl.ds((z + k) * (n + PAD), n), :] = value[:, k * n : (k + 1) * n]
        return carry

    lax.fori_loop(0, n // STEP, forward, 0)

    def columns(i, carry):
        y = i * STEP
        value = jnp.concatenate([work[pl.ds(y + k, n, stride=n + PAD), :] for k in range(STEP)], 1)
        value = table_times(left, value)
        base = gz_ref[...] + (gx_ref[...] + KAPPA_SQ)
        value = jnp.concatenate(
            [
                value[:, k * n : (k + 1) * n] * (scale / (base + gz_ref[pl.ds(y + k, 1), :]))
                for k in range(STEP)
            ],
            1,
        )
        value = table_times(left, value)
        for k in range(STEP):
            work[pl.ds(y + k, n, stride=n + PAD), :] = value[:, k * n : (k + 1) * n]
        return carry

    lax.fori_loop(0, n // STEP, columns, 0)

    def backward(i, carry):
        turn = i // steps
        half = slots // 2
        slot = jnp.where(turn < half, 2 * turn + 1, 2 * (turn - half))
        if last:

            @pl.when(i % steps == 0)
            def _():
                old_copy(slot).wait()

        z = (slot * steps + i % steps) * STEP
        value = jnp.concatenate([work[pl.ds((z + k) * (n + PAD), n), :] for k in range(STEP)], 1)
        value = times_table(below(table_times(left, value), STEP), right).reshape(STEP, n, n)
        value = value * (src[pl.ds(z, STEP)] * weight)
        if last:
            value = value + acc[pl.ds(z, STEP)]
        acc[pl.ds(z, STEP)] = value
        for done in range(slots):

            @pl.when((i % steps == steps - 1) & (slot == done))
            def _(done=done):
                for copy in out_copies(done):
                    copy.start()

        return carry

    lax.fori_loop(0, n // STEP, backward, 0)
    for slot in range(slots):
        for copy in out_copies(slot):
            copy.wait()


def exchange(where, occ, res_pieces, src_pieces, old, tables, waves):
    right, left = tables
    slots = len(res_pieces[0])
    slab_len, n, _ = res_pieces[0][0].shape
    last = old is not None
    any_spec = pl.BlockSpec(memory_space=pl.ANY)
    vmem_spec = pl.BlockSpec(memory_space=pltpu.VMEM)
    smem_spec = pl.BlockSpec(memory_space=pltpu.SMEM)
    layout = [place for _, *place in src_pieces]
    arrays = [*res_pieces[0], *res_pieces[1], *[array for array, *_ in src_pieces]]
    if last:
        arrays.append(old)
        shapes = [(slots, slab_len, n, n), (slots // 2, slab_len, n, n), (slots // 2, slab_len, n, n)]
    else:
        shapes = [(n, n, n)]
    return pl.pallas_call(
        functools.partial(exchange_kernel, n, slots, layout, last),
        out_shape=[jax.ShapeDtypeStruct(shape, F32) for shape in shapes],
        in_specs=[smem_spec] * 2 + [vmem_spec] * 4 + [any_spec] * len(arrays),
        out_specs=[any_spec] * len(shapes),
        scratch_shapes=[
            pltpu.VMEM((n, n, n), F32),
            pltpu.VMEM((n, n, n), F32),
            pltpu.VMEM((n * (n + PAD) + n, n), F32),
            pltpu.VMEM((n, n, n), F32),
            pltpu.SemaphoreType.DMA((2, slots)),
            pltpu.SemaphoreType.DMA((slots, 2, PARTS)),
            pltpu.SemaphoreType.DMA((slots,)),
            pltpu.SemaphoreType.DMA((slots, 2)),
        ],
        compiler_params=pltpu.CompilerParams(vmem_limit_bytes=48 * 2**20),
        cost_estimate=pl.CostEstimate(
            flops=72 * n**4, bytes_accessed=4 * n**3 * (5 if last else 3), transcendentals=0
        ),
        name="exchange",
    )(where, occ.reshape(1), waves[None, :], jnp.broadcast_to(waves[:, None], (n, n)), right, left, *arrays)


def whole_grids(resident, blocks, occupation):
    count_res, slab_len, n, _ = resident.shape
    planes = lax.axis_size("slab") // 2
    names = ("band", "slab")
    coords = [
        (x, c, z, y) for x in range(2) for c in range(2) for z in range(planes) for y in range(2)
    ]

    def flat(x, c, z, y):
        return ((x * 2 + c) * planes + z) * 2 + y

    def send(value, rule):
        pairs = []
        for coord in coords:
            target = rule(*coord)
            if target is not None:
                pairs.append((flat(*coord), flat(*target)))
        return lax.ppermute(value, names, pairs)

    band, slab = (lax.axis_index("band"), lax.axis_index("slab"))
    c, z, y = (band % 2, slab // 2, slab % 2)

    def swap_x(v):
        return send(v, lambda x, c, z, y: (1 - x, c, z, y))

    def swap_c(v):
        return send(v, lambda x, c, z, y: (x, 1 - c, z, y))

    def swap_y(v):
        return send(v, lambda x, c, z, y: (x, c, z, 1 - y))

    def turn_cy(v):
        return send(v, lambda x, c, z, y: (x, y, z, c))

    def pick(values, index):
        out = values[0]
        for k in range(1, len(values)):
            out = jnp.where(index == k, values[k], out)
        return out

    part_len = slab_len // PARTS
    own = []
    for part in range(PARTS):
        rows = slice(part * part_len, (part + 1) * part_len)
        quads = [lax.dynamic_index_in_dim(blocks, band, 0, False)[rows]]
        for other in range(1, 4):
            dx, dc = (other // 2, other % 2)
            value = lax.dynamic_index_in_dim(blocks, band ^ other, 0, False)[rows]
            quads.append(send(value, lambda x, c, z, y, dx=dx, dc=dc: (x ^ dx, c ^ dc, z, y)))
        slots = [pick(quads, z ^ band)]
        for step in range(1, planes):
            value = pick(quads, ((z + step) % planes) ^ band)
            slots.append(send(value, lambda x, c, z, y, step=step: (x, c, (z + step) % planes, y)))
        own.append(jnp.stack([slots[0], *slots[:0:-1]]))

    residents = []
    for r in range(count_res):
        piece = turn_cy(resident[r])
        downs, ups = ([], [])
        down = up = piece
        for step in range(1, planes):
            if r == 0 and step == 2:
                down, up, _ = lax.optimization_barrier((down, up, own[-1]))
            if r > 0 and step == 1:
                down, up, earlier = lax.optimization_barrier((down, up, earlier))
            down = send(down, lambda x, c, z, y: (x, c, z - 1, y) if 1 <= z <= planes - step else None)
            up = send(up, lambda x, c, z, y: (x, c, z + 1, y) if step - 1 <= z < planes - 1 else None)
            downs.append(down)
            ups.append(up)
        earlier = downs[1]
        slots = [piece]
        for step in range(1, planes):
            slots.append(jnp.where(z + step < planes, downs[step - 1], ups[planes - step - 1]))
        residents.append([slots, [swap_c(v) for v in slots]])

    near, far = ([], [])
    half = planes // 2
    for part in range(PARTS):
        beside_y = swap_y(own[part])
        beside_x = swap_x(own[part])
        low = swap_y(beside_x[:half])
        high = swap_x(beside_y[half:])
        near += [(own[part], 0, planes, 0, part), (beside_y, 0, planes, 1, part)]
        far += [
            (beside_x, 0, planes, 0, part),
            (low, 0, half, 1, part),
            (high, half, half, 1, part),
        ]

    occ = [lax.dynamic_index_in_dim(occupation, 4 * z + (band ^ other), 0, False) for other in (0, 2)]
    where = jnp.stack([c, y]).astype(jnp.int32)
    waves = wave_of(jnp.arange(n, dtype=jnp.int32), n) ** 2
    tables = cas_tables(n)
    rows, ties = ([], [where, where])
    for r in range(count_res):
        (old,) = exchange(ties[0], occ[0], residents[r], near, None, tables, waves)
        keep, odd, even = exchange(ties[1], occ[1], residents[r], far, old, tables, waves)
        odd, even = (swap_c(odd), swap_c(even))

        terms = {}
        for part, array in ((1, odd), (0, even)):
            slots = range(part, planes, 2)
            sums = [keep[slot] + array[slot // 2] for slot in slots]
            terms.update(zip(slots, lax.optimization_barrier(sums)))

        down = up = None
        for step in range(1, planes):
            low, high = (terms[step], terms[planes - step])
            if step > 1:
                low, high = (low + down, high + up)
            if r + 1 < count_res and step < planes - 1:
                low, high, ties[step - 1] = lax.optimization_barrier((low, high, where))
            down = send(low, lambda x, c, z, y: (x, c, z - 1, y) if z >= max(planes - step, 1) else None)
            up = send(high, lambda x, c, z, y: (x, c, z + 1, y) if z <= min(step - 1, planes - 2) else None)
        rows.append(turn_cy(terms[0] + down + up))
    return jnp.stack(rows)


def per_device(resident, blocks, occupation):
    if (
        lax.axis_size("band") == 4
        and lax.axis_size("slab") == 8
        and resident.shape[0] == 2
        and blocks.shape[0] == 4
        and 2 * resident.shape[1] % STEP == 0
    ):
        return whole_grids(resident, blocks, occupation)
    return sliced_grids(resident, blocks, occupation)


def solution(mesh):
    placed = (P("band", "slab", None, None), P("band", "slab", None, None), P())
    return jax.shard_map(
        per_device,
        mesh=mesh,
        in_specs=placed,
        out_specs=P("band", "slab", None, None),
        check_vma=False,
    )
```
